512 devices in a mesh: dp: 2 (over core), ctx: 32 (over x, y), tp: 8 (over z).
Axes of the slice: x: 4, y: 8, z: 8, core: 2. Of those that a mesh axis runs over, the one named last changes fastest.
Arguments:
- x_in: bfloat16 [2, 16384, 8192], P('dp', 'ctx', 'tp'), may hold values from -6 to 6
- grad_out: bfloat16 [2, 16384, 8192], P('dp', 'ctx', 'tp'), may hold values from -16 to 16
- state_maps: bfloat16 [2, 16384, 256], P('dp', 'ctx'), may hold values from -0.875 to 0.875
- dt_raw: float32 [2, 128, 16384], P('dp', 'tp', 'ctx'), may hold values from -3 to 20
- a_log: float32 [128], P('tp'), may hold values from -12 to 0
- saved_states: float32 [2, 32, 128, 64, 128], P('dp', 'ctx', 'tp'), may hold values from -0.625 to 0.625
- layer_in: bfloat16 [2, 16384, 8192], P('dp', 'ctx', 'tp'), may hold values from -40 to 40
- doc_lengths: int32 [2, 4], P('dp'), may hold values from 1 to 8192, 16384 in all within a row
Outputs:
- grad_x: bfloat16 [2, 16384, 8192], P('dp', 'ctx', 'tp')
- grad_maps: float32 [2, 16384, 256], P('dp', ('ctx', 'tp'))
- grad_dt_proj: float32 [128, 8192], P(('dp', 'ctx'), 'tp')
The draws below stay inside these ranges and needn't reach their ends.
All inputs are finite; a program needn't handle non-finite values.
Results may differ from the reference program's by a relative error of at most 0.0055.
Values may be sent and summed in bfloat16 or wider, within the bound.
No kernel may reach another device: no remote copies, remote signals or barrier semaphores. Data moves between devices by JAX's collectives and lax.ppermute only.
A program may use at most 128 MiB of HBM per device.

```python
import math
import jax
import jax.numpy as jnp
import numpy as np
from jax import lax

D = 8192
HEADS = 128
HEAD_DIM = 64
STATE = 128
TOK_DEV = 512
DOCS = 4
BATCH_SEQUENCES = 2
BLOCKS = 32
SEQUENCE_LENGTH = 16384


def decay_plan(key):
    random_subkey_list = jax.random.split(key, 4)
    slow_share = 0.5
    slow_heads = jax.random.uniform(random_subkey_list[0], (HEADS,)) < slow_share
    slow_rate = jnp.exp(jax.random.uniform(random_subkey_list[1], (HEADS,), minval=math.log(0.2), maxval=math.log(0.8))) / SEQUENCE_LENGTH
    fast_rate = jnp.exp(jax.random.uniform(random_subkey_list[2], (HEADS,), minval=math.log(0.02), maxval=math.log(0.05)))
    decay_rate = jnp.where(slow_heads, slow_rate, fast_rate)
    default_step_size = jnp.exp(jax.random.uniform(random_subkey_list[3], (HEADS,), minval=math.log(0.2), maxval=math.log(0.6)))
    return (decay_rate, default_step_size)


def draw_a_log(key, part):
    decay_rate, default_step_size = decay_plan(jax.random.fold_in(key, 11))
    return jnp.log(decay_rate / default_step_size).astype(jnp.float32)


def draw_dt_raw(key, part):
    decay_rate, default_step_size = decay_plan(jax.random.fold_in(key, 11))
    random_subkey_list = jax.random.split(jax.random.fold_in(key, 12), 3)
    block_count = SEQUENCE_LENGTH // TOK_DEV
    block_multiplier = jnp.exp(jax.random.uniform(random_subkey_list[0], (BATCH_SEQUENCES, HEADS, block_count), minval=-math.log(2.0), maxval=math.log(2.0)))
    block_multiplier = jnp.repeat(block_multiplier, TOK_DEV, axis=2)
    token_multiplier = jnp.exp(jax.random.uniform(random_subkey_list[1], (BATCH_SEQUENCES, HEADS, SEQUENCE_LENGTH), minval=-math.log(2.0), maxval=math.log(2.0)))
    spike_events = jax.random.uniform(random_subkey_list[2], (BATCH_SEQUENCES, 1, SEQUENCE_LENGTH)) < 4.0 / SEQUENCE_LENGTH
    spike_increase = jnp.where(spike_events, 8.0, 1.0)
    step_sizes_delta = default_step_size[None, :, None] * block_multiplier * token_multiplier * spike_increase
    return jnp.log(jnp.expm1(step_sizes_delta)).astype(jnp.float32)


def draw_grad_out(key, part):
    columns = HEADS * HEAD_DIM
    head_index = (jnp.arange(columns) // HEAD_DIM).astype(jnp.float32)
    random_subkey_list = jax.random.split(key, 1)
    head_scale = 0.5 * (1.0 + 2.0 * head_index / (HEADS - 1))
    drawn = jax.random.truncated_normal(random_subkey_list[0], -4.0, 4.0, (BATCH_SEQUENCES, SEQUENCE_LENGTH, columns)) * head_scale
    return drawn.astype(jnp.bfloat16)


def draw_layer_in(key, part):
    fraction = jnp.arange(D).astype(jnp.float32) / D
    random_subkey_list = jax.random.split(key, 1)
    column_scale = 0.3 * jnp.power(10.0, fraction)
    drawn = jax.random.truncated_normal(random_subkey_list[0], -4.0, 4.0, (BATCH_SEQUENCES, SEQUENCE_LENGTH, D)) * column_scale
    return drawn.astype(jnp.bfloat16)


def block_levels(rng, dims, cuts, low, high):
    level, own = 1.0, jax.random.fold_in(rng, 6)
    for axis_at, blocks in cuts:
        steps = jnp.exp(jax.random.uniform(jax.random.fold_in(own, axis_at), (blocks,), jnp.float32, low / len(cuts), high / len(cuts)))
        level = level * jnp.repeat(steps, dims[axis_at] // blocks).reshape([-1 if axis == axis_at else 1 for axis in range(len(dims))])
    return level


def split_up(count, total, reach, slope):
    weights = [(1 << 20) // math.isqrt(grade ** slope) + 1 for grade in range(2, count + 1)]
    surplus, given = total - reach - (count - 1), [1] * (count - 1)
    while surplus > 0:
        candidates = [i for i in range(count - 1) if given[i] < reach]
        whole, remaining = sum([weights[i] for i in candidates]), surplus
        for i in candidates:
            more = min(reach - given[i], max(1, remaining * weights[i] // whole), surplus)
            given[i] = given[i] + more
            surplus = surplus - more
    return np.array([reach] + given)


def uneven_parts(own_key, count, total, most, slope):
    if count == 2:
        one = jax.random.randint(own_key, (), max(1, total - most), min(most, total - 1) + 1)
        return jnp.stack([one, total - one])
    lengths = jnp.asarray(split_up(count, total, most, slope), jnp.int32)
    pairs = (count - 1) // 2
    donor, taker = lengths[1:1 + 2 * pairs:2], lengths[2:2 + 2 * pairs:2]
    margin = jnp.minimum(donor - 1, most - taker)
    moved = jax.random.randint(jax.random.fold_in(own_key, 1), (pairs,), 0, 1 << 20) % (margin + 1)
    lengths = lengths.at[1:1 + 2 * pairs:2].set(donor - moved).at[2:2 + 2 * pairs:2].set(taker + moved)
    return lengths[jax.random.permutation(jax.random.fold_in(own_key, 2), count)]


def gaussian(key, extent, deviation, reach, pieces=(), kind=jnp.bfloat16):
    entries = jax.random.normal(key, extent, jnp.float32) * deviation
    if len(pieces) > 0:
        entries = block_levels(key, extent, pieces, -0.22, 0.18) * entries
    return jnp.clip(entries, min=-reach, max=reach).astype(kind)


def setup_inputs(seed: int = 0) -> dict:
    seeds = jax.random.split(jax.random.key(seed), 9)
    return {
        "x_in": gaussian(seeds[0], (BATCH_SEQUENCES, SEQUENCE_LENGTH, HEADS * HEAD_DIM), 1.0, 6.0, ((0, 2), (1, 32), (2, 8))),
        "grad_out": draw_grad_out(jax.random.fold_in(seeds[8], 71), 0),
        "state_maps": gaussian(seeds[2], (BATCH_SEQUENCES, SEQUENCE_LENGTH, 2 * STATE), 0.15, 0.875, ((0, 2), (1, 32))),
        "dt_raw": draw_dt_raw(jax.random.fold_in(seeds[8], 71), 0),
        "a_log": draw_a_log(jax.random.fold_in(seeds[8], 71), 0),
        "saved_states": gaussian(seeds[5], (BATCH_SEQUENCES, BLOCKS, HEADS, HEAD_DIM, STATE), 0.1, 0.625, ((0, 2), (1, 32), (2, 8)), jnp.float32),
        "layer_in": draw_layer_in(jax.random.fold_in(seeds[8], 71), 0),
        "doc_lengths": jax.vmap(lambda own: uneven_parts(own, DOCS, SEQUENCE_LENGTH, SEQUENCE_LENGTH // 2, 2))(jax.random.split(seeds[7], BATCH_SEQUENCES)).reshape((BATCH_SEQUENCES, DOCS)).astype(jnp.int32),
    }


head_group = 4
epsilon = 1e-06

def block_setup(raw_steps, a_log, labels, before):
    step_sizes_delta = jax.nn.softplus(raw_steps)
    decay_rate = -jnp.exp(a_log)
    cumulative = jnp.cumsum(decay_rate[:, None] * step_sizes_delta, axis=1)
    enter_w = jnp.exp(cumulative) * (labels == before).astype(jnp.float32)[None, :]
    leave_w = jnp.exp(cumulative[:, -1:] - cumulative) * (labels == labels[-1]).astype(jnp.float32)[None, :]
    return (step_sizes_delta, decay_rate, cumulative, enter_w, leave_w)

def first_pass(dy_rows, c_rows, enter_w):
    scaled = (jnp.transpose(enter_w)[:, :, None] * dy_rows.astype(jnp.float32)).astype(jnp.bfloat16)
    local_grad = jnp.einsum('ihp,in->hpn', scaled.astype(jnp.float32), c_rows.astype(jnp.float32), precision=lax.Precision.HIGHEST)
    return (scaled, local_grad)

def quad_terms(cumulative, step_sizes_delta, x_rows, dy_rows, pair_dot, causal):
    length, head_count, head_width = x_rows.shape
    highest = lax.Precision.HIGHEST

    def one_group(group_index, running):
        mixed_sum, r_local, dc_local = running
        offset = group_index * head_group
        c_part = lax.dynamic_slice_in_dim(cumulative, offset, head_group, 0)
        d_part = lax.dynamic_slice_in_dim(step_sizes_delta, offset, head_group, 0)
        x_part = lax.dynamic_slice_in_dim(x_rows, offset, head_group, 1)
        y_part = lax.dynamic_slice_in_dim(dy_rows, offset, head_group, 1)
        log_diffs = c_part[:, :, None] - c_part[:, None, :]
        kernel = jnp.where(causal[None], jnp.exp(jnp.where(causal[None], log_diffs, 0.0)), 0.0)
        weighted = kernel * pair_dot[None]
        rounded = weighted.astype(jnp.bfloat16)
        inner_dt = jnp.einsum('ihp,jhp->hij', y_part.astype(jnp.float32), x_part.astype(jnp.float32), precision=highest) * d_part[:, None, :]
        r_part = jnp.einsum('hij,ihp->jhp', rounded.astype(jnp.float32), y_part.astype(jnp.float32), precision=highest)
        products = weighted * inner_dt
        dc_part = lax.optimization_barrier(jnp.sum(products, axis=2)) - lax.optimization_barrier(jnp.sum(products, axis=1))
        mixed_sum = mixed_sum + lax.optimization_barrier(jnp.sum(kernel * inner_dt, axis=0))
        r_local = lax.dynamic_update_slice_in_dim(r_local, r_part, offset, 1)
        dc_local = lax.dynamic_update_slice_in_dim(dc_local, dc_part, offset, 0)
        return (mixed_sum, r_local, dc_local)
    initial = (jnp.zeros((length, length), jnp.float32), jnp.zeros((length, head_count, head_width), jnp.float32), jnp.zeros((head_count, length), jnp.float32))
    return lax.fori_loop(0, head_count // head_group, one_group, initial)

def block_grads(x_rows, dy_rows, map_rows, raw_steps, labels, before, states, carried, a_log):
    highest = lax.Precision.HIGHEST
    length = x_rows.shape[0]
    b_rows = map_rows[:, :STATE].astype(jnp.float32)
    c_rows = map_rows[:, STATE:].astype(jnp.float32)
    step_sizes_delta, decay_rate, cumulative, enter_w, leave_w = block_setup(raw_steps, a_log, labels, before)
    scaled, local_grad = first_pass(dy_rows, map_rows[:, STATE:], enter_w)
    positions = jnp.arange(length)
    causal = (positions[:, None] >= positions[None, :]) & (labels[:, None] == labels[None, :])
    pair_dot = jnp.dot(c_rows, b_rows.T, preferred_element_type=jnp.float32, precision=highest)
    mixed_sum, r_local, dc_local = quad_terms(cumulative, step_sizes_delta, x_rows, dy_rows, pair_dot, causal)
    state_term = jnp.einsum('ihp,hpn->in', scaled.astype(jnp.float32), states, precision=highest)
    local_b = jnp.einsum('ij,in->jn', mixed_sum, c_rows, precision=highest)
    local_c = jnp.einsum('ij,jn->in', mixed_sum, b_rows, precision=highest) + state_term
    state_c = jnp.einsum('in,hpn->ihp', c_rows, states, precision=highest)
    enter_out = enter_w * jnp.einsum('ihp,ihp->hi', dy_rows.astype(jnp.float32), state_c, precision=highest)
    carry_b = jnp.einsum('jn,hpn->jhp', b_rows, carried, precision=highest)
    carry_r = jnp.transpose(leave_w)[:, :, None] * carry_b
    r_all = r_local + carry_r
    x_wide = x_rows.astype(jnp.float32)
    weighted_x = jnp.transpose(step_sizes_delta * leave_w)[:, :, None] * x_wide
    carry_bgrad = jnp.einsum('jhp,hpn->jn', weighted_x, carried, precision=highest)
    grad_x = (jnp.transpose(step_sizes_delta)[:, :, None] * r_all).astype(jnp.bfloat16)
    w_term = step_sizes_delta * jnp.einsum('jhp,jhp->hj', x_wide, carry_r, precision=highest)
    v_term = enter_w[:, -1] * lax.optimization_barrier(jnp.sum(carried * states, axis=(1, 2)))
    last_mask = (positions == length - 1).astype(jnp.float32)
    cum_grad = dc_local + enter_out - w_term + (v_term + lax.optimization_barrier(jnp.sum(w_term, axis=1)))[:, None] * last_mask[None, :]
    tail_sum = jnp.flip(jnp.cumsum(jnp.flip(cum_grad, 1), axis=1), 1)
    step_grad = jnp.einsum('jhp,jhp->hj', x_wide, r_all, precision=highest) + decay_rate[:, None] * tail_sum
    dt_grad = (step_grad * jax.nn.sigmoid(raw_steps)).astype(jnp.bfloat16)
    grad_maps = jnp.concatenate([local_b + carry_bgrad, local_c], axis=1)
    return (grad_x.reshape(length, -1), grad_maps, dt_grad)

def reference(x_in, grad_out, state_maps, dt_raw, a_log, saved_states, layer_in, doc_lengths):
    grads_x = []
    grads_maps = []
    dt_grads = []
    for replica in range(BATCH_SEQUENCES):
        doc_ends = jnp.cumsum(doc_lengths[replica]).astype(jnp.int32)
        positions = jnp.arange(SEQUENCE_LENGTH, dtype=jnp.int32)
        labels_all = lax.optimization_barrier(jnp.sum((positions[:, None] >= doc_ends[None, :]).astype(jnp.int32), axis=1)).astype(jnp.int32)
        prior_label = jnp.concatenate([jnp.full((1,), -1, jnp.int32), labels_all[:-1]])
        x_blocks = x_in[replica].reshape(BLOCKS, TOK_DEV, HEADS, HEAD_DIM)
        dy_blocks = grad_out[replica].reshape(BLOCKS, TOK_DEV, HEADS, HEAD_DIM)
        map_blocks = state_maps[replica].reshape(BLOCKS, TOK_DEV, 2 * STATE)
        raw_blocks = jnp.transpose(dt_raw[replica].reshape(HEADS, BLOCKS, TOK_DEV), (1, 0, 2))
        label_blocks = labels_all.reshape(BLOCKS, TOK_DEV)
        before_all = prior_label.reshape(BLOCKS, TOK_DEV)[:, 0]

        def section_one(payload):
            dy_rows, map_rows, raw_steps, labels, before = payload
            step_sizes_delta, decay_rate, cumulative, enter_w, leave_w = block_setup(raw_steps, a_log, labels, before)
            scaled, local_grad = first_pass(dy_rows, map_rows[:, STATE:], enter_w)
            return (enter_w[:, -1], local_grad)
        decay_ends, local_grads = lax.map(section_one, (dy_blocks, map_blocks, raw_blocks, label_blocks, before_all))

        def link_back(carried, payload):
            decay_end, local_grad = payload
            return (local_grad + decay_end[:, None, None] * carried, carried)
        zero_state = jnp.zeros((HEADS, HEAD_DIM, STATE), jnp.float32)
        unused, carries = lax.scan(link_back, zero_state, (decay_ends, local_grads), reverse=True)

        def section_two(payload):
            x_rows, dy_rows, map_rows, raw_steps, labels, before, states, carried = payload
            return block_grads(x_rows, dy_rows, map_rows, raw_steps, labels, before, states, carried, a_log)
        block_x, block_maps, block_dt = lax.map(section_two, (x_blocks, dy_blocks, map_blocks, raw_blocks, label_blocks, before_all, saved_states[replica], carries))
        grads_x.append(block_x.reshape(SEQUENCE_LENGTH, HEADS * HEAD_DIM))
        grads_maps.append(block_maps.reshape(SEQUENCE_LENGTH, 2 * STATE))
        dt_grads.append(block_dt)
    grad_x = jnp.stack(grads_x)
    grad_maps = jnp.stack(grads_maps)
    dt_all = jnp.stack(dt_grads).reshape(BATCH_SEQUENCES * BLOCKS, HEADS, TOK_DEV)
    layer_blocks = layer_in.reshape(BATCH_SEQUENCES * BLOCKS, TOK_DEV, D)

    def accumulate(running, payload):
        dt_part, layer_part = payload
        added = jnp.dot(dt_part.astype(jnp.float32), layer_part.astype(jnp.float32), preferred_element_type=jnp.float32, precision=lax.Precision.HIGHEST)
        return (running + added, None)
    summed, unused = lax.scan(accumulate, jnp.zeros((HEADS, D), jnp.float32), (dt_all, layer_blocks))
    norms = jnp.sqrt(lax.optimization_barrier(jnp.sum(summed * summed, axis=1)) + epsilon)
    target = jnp.mean(norms)
    grad_dt_proj = summed * jnp.minimum(1.0, target / norms)[:, None]
    return (grad_x, grad_maps, grad_dt_proj)
```

```python
import jax
import jax.numpy as jnp
from jax import lax
from jax.experimental import pallas as pl
from jax.experimental.pallas import tpu as pltpu
from jax.sharding import Mesh
from jax.sharding import PartitionSpec as P

HEAD_DIM = 64
STATE = 128
SUB = 128
CTX = ("ctx_0", "ctx_1")
DP_CTX = ("dp", "ctx_0", "ctx_1")
CTX_TP = ("ctx_0", "ctx_1", "tp")
epsilon = 1e-06
NEG = -1e30

f32 = jnp.float32
bf16 = jnp.bfloat16
VMEM = pl.BlockSpec(memory_space=pltpu.VMEM)
SMEM = pl.BlockSpec(memory_space=pltpu.SMEM)


def dot(a, b, ca, cb):
    return lax.dot_general(a, b, (((ca,), (cb,)), ((), ())), preferred_element_type=f32)


def iota(shape, dim):
    return lax.broadcasted_iota(jnp.int32, shape, dim)


def doc_ends(docs):
    ends, total = [], 0
    for k in range(docs.shape[1]):
        total = total + docs[0, k]
        ends.append(total)
    return ends


def label_of(position, ends):
    label = 0
    for end in ends:
        label = label + jnp.where(position >= end, 1, 0)
    return label


def label_before(anchor, ends):
    return jnp.where(anchor > 0, label_of(anchor - 1, ends), -1)


def running(x, reverse=False):
    length = x.shape[1]
    lane = iota(x.shape, 1)
    step = 1
    while step < length:
        if reverse:
            x = x + jnp.where(lane < length - step, pltpu.roll(x, length - step, 1), 0.0)
        else:
            x = x + jnp.where(lane >= step, pltpu.roll(x, step, 1), 0.0)
        step *= 2
    return x


def steps_of(raw, a_log, heads):
    step = jnp.maximum(raw, 0.0) + jnp.log1p(jnp.exp(-jnp.abs(raw)))
    row = iota((heads, 1), 0)
    column = jnp.zeros((heads, 1), f32)
    for h in range(heads):
        column = jnp.where(row == h, a_log[h], column)
    rate = jnp.exp(column)
    return step, rate, -running(rate * step)


def split_two(x):
    high = x.astype(bf16)
    return high, (x - high.astype(f32)).astype(bf16)


def tall(x):
    high = x.astype(bf16).astype(f32)
    return jnp.transpose(jnp.concatenate([high, x - high], axis=0)).astype(bf16)


def spread_matrix(heads):
    shape = (2 * heads, heads * HEAD_DIM)
    return jnp.where(iota(shape, 1) // HEAD_DIM == iota(shape, 0) % heads, 1.0, 0.0).astype(bf16)


def gather_matrix(heads):
    shape = (heads, heads * HEAD_DIM)
    return jnp.where(iota(shape, 1) // HEAD_DIM == iota(shape, 0), 1.0, 0.0).astype(bf16)


def first_kernel(docs, anchor, a_log, raw, dy, maps, out):
    heads, length = raw.shape
    ends = doc_ends(docs)
    labels = label_of(anchor[0] + iota((1, length), 1), ends)
    step, rate, cum = steps_of(raw[...], a_log, heads)
    enter = jnp.where(labels == label_before(anchor[0], ends), jnp.exp(cum), 0.0)
    scaled = (dot(tall(enter), spread_matrix(heads), 1, 0) * dy[...].astype(f32)).astype(bf16)
    local = dot(scaled, maps[:, STATE:], 0, 0).astype(bf16)
    last = jnp.broadcast_to(enter[:, length - 1 :], (heads, STATE))
    high = last.astype(bf16).astype(f32)
    low = last - high
    row = iota((8, STATE), 0)
    rows = out.shape[1] - 8
    per_head = HEAD_DIM // rows
    for h in range(heads):
        tail = jnp.where(row == 0, high[h : h + 1], jnp.where(row == 1, low[h : h + 1], 0.0))
        for part in range(per_head):
            start = h * HEAD_DIM + part * rows
            out[h * per_head + part, :rows, :] = local[start : start + rows]
            out[h * per_head + part, rows:, :] = tail.astype(bf16)


def scan_kernel(pieces, out):
    blocks, rows = out.shape[:2]
    carry = jnp.zeros(out.shape[1:], f32)
    for k in reversed(range(blocks)):
        out[k] = carry.astype(bf16)
        if k:
            tail = pieces[k, rows:, :].astype(f32)
            carry = pieces[k, :rows, :].astype(f32) + (tail[0:1] + tail[1:2]) * carry


def quad_kernel(
    docs, anchor, a_log, raw, x, dy, maps, states,
    rdt_out, xl_out, gm_out, vec_out,
    ye, yo, xe, xo, sa, sb, sc, dte, gae, gbe, ua, ub, zs, dd, pb, ms, cum_tall, tl,
):
    heads, length = raw.shape
    wide = x.shape[1]
    half, quarter = length // 2, length // 4
    ends = doc_ends(docs)
    base = anchor[0]
    position = iota((1, length), 1)
    labels = label_of(base + position, ends)
    step, rate, cum = steps_of(raw[...], a_log, heads)
    enter = jnp.where(labels == label_before(base, ends), jnp.exp(cum), 0.0)
    leave = jnp.where(
        labels == label_of(base + length - 1, ends), jnp.exp(cum[:, length - 1 :] - cum), 0.0
    )
    toward_a = jnp.where(position < half, 1.0, -1.0)
    mid = cum[:, half - 1 : half]
    scale_a = jnp.where(
        labels == label_of(base + half - 1, ends), jnp.exp((mid - cum) * toward_a), 0.0
    )
    low_half = position < half
    first = (position // quarter) % 2 == 0
    toward_b = jnp.where(first, 1.0, -1.0)
    edge = jnp.where(
        low_half, cum[:, quarter - 1 : quarter], cum[:, half + quarter - 1 : half + quarter]
    )
    edge_label = jnp.where(
        low_half, label_of(base + quarter - 1, ends), label_of(base + half + quarter - 1, ends)
    )
    scale_b = jnp.where(labels == edge_label, jnp.exp((edge - cum) * toward_b), 0.0)
    cum_tall[...] = jnp.transpose(cum)
    for k, scale in enumerate((step, enter, leave, scale_a, scale_b)):
        tl[k] = tall(scale)

    spread = spread_matrix(heads)
    lane = iota((1, wide), 1)
    even = jnp.where((lane // HEAD_DIM) % 2 == 0, 1.0, 0.0).astype(bf16)
    odd = jnp.where((lane // HEAD_DIM) % 2 == 1, 1.0, 0.0).astype(bf16)

    for d in range(4):
        rows = slice(d * quarter, (d + 1) * quarter)
        yb = dy[rows, :]
        yv = yb.astype(f32)
        dt_e = dot(tl[0, rows, :], spread, 1, 0)
        dte[rows, :] = dt_e
        xdt = (dt_e * x[rows, :].astype(f32)).astype(bf16)
        xv = xdt.astype(f32)
        xe[rows, :] = xdt * even
        xo[rows, :] = xdt * odd
        ye[rows, :] = yb * even
        yo[rows, :] = yb * odd
        sc[rows, :] = (dot(tl[1, rows, :], spread, 1, 0) * yv).astype(bf16)
        xl_out[rows, :] = (dot(tl[2, rows, :], spread, 1, 0) * xv).astype(bf16)
        ga = dot(tl[3, rows, :], spread, 1, 0)
        gb = dot(tl[4, rows, :], spread, 1, 0)
        sa[rows, :] = (ga * (xv if d < 2 else yv)).astype(bf16)
        sb[rows, :] = (gb * (xv if d % 2 == 0 else yv)).astype(bf16)
        if d < 2:
            gae[rows, :] = ga
        if d % 2 == 0:
            gbe[rows, :] = gb

    ms[...] = jnp.zeros(ms.shape, bf16)
    lower, upper = slice(0, half), slice(half, length)
    cba = dot(maps[upper, STATE:], maps[lower, :STATE], 1, 1).astype(bf16)
    ua[lower, :] = dot(cba, sa[upper, :], 0, 0)
    ua[upper, :] = dot(cba, sa[lower, :], 1, 0)
    ms[upper, lower] = dot(sa[upper, :], sa[lower, :], 1, 1).astype(bf16)
    for q in range(2):
        lower = slice(2 * q * quarter, (2 * q + 1) * quarter)
        upper = slice((2 * q + 1) * quarter, (2 * q + 2) * quarter)
        cbb = dot(maps[upper, STATE:], maps[lower, :STATE], 1, 1).astype(bf16)
        ub[lower, :] = dot(cbb, sb[upper, :], 0, 0)
        ub[upper, :] = dot(cbb, sb[lower, :], 1, 0)
        ms[upper, lower] = dot(sb[upper, :], sb[lower, :], 1, 1).astype(bf16)
    sv = states[...].astype(bf16)
    zs[...] = dot(maps[:, STATE:], sv, 1, 1)

    ri, rj = iota((quarter, quarter), 0), iota((quarter, quarter), 1)
    for d in range(4):
        rows = slice(d * quarter, (d + 1) * quarter)
        at = base + d * quarter
        keep = (ri >= rj) & (label_of(at + ri, ends) == label_of(at + rj, ends))
        cb = dot(maps[rows, STATE:], maps[rows, :STATE], 1, 1)
        mask = jnp.where(keep, 0.0, NEG)
        total = jnp.zeros((quarter, quarter), f32)
        for pair in range(heads // 2):
            cols = slice(pair * 2 * HEAD_DIM, (pair + 1) * 2 * HEAD_DIM)
            y2 = jnp.concatenate([ye[rows, cols], yo[rows, cols]], axis=0)
            x2 = jnp.concatenate([xe[rows, cols], xo[rows, cols]], axis=0)
            xp = xe[rows, cols] + xo[rows, cols]
            inner = dot(y2, xp, 1, 1)
            weights = []
            for s in range(2):
                h = 2 * pair + s
                gap = cum_tall[rows, h : h + 1] - cum[h : h + 1, rows]
                kernel = jnp.exp(gap + mask)
                total = total + kernel * inner[s * quarter : (s + 1) * quarter]
                weights.append((kernel * cb).astype(bf16))
            r = dot(jnp.concatenate(weights, axis=0), y2, 0, 0)
            o = dot(jnp.concatenate(weights, axis=1), x2, 1, 0)
            yv = dy[rows, cols].astype(f32)
            back = xp.astype(f32) * r
            fore = yv * o + sc[rows, cols].astype(f32) * zs[rows, cols]
            ta = sa[rows, cols].astype(f32) * ua[rows, cols]
            tb = sb[rows, cols].astype(f32) * ub[rows, cols]
            if d < 2:
                back = back + ta
                r = r + gae[rows, cols] * ua[rows, cols]
            else:
                fore = fore + ta
            if d % 2 == 0:
                back = back + tb
                r = r + gbe[rows, cols] * ub[rows, cols]
            else:
                fore = fore + tb
            rdt_out[rows, cols] = dte[rows, cols] * r
            pb[rows, cols] = back.astype(bf16)
            dd[rows, cols] = fore - back
        ms[rows, rows] = total.astype(bf16)

    collect = gather_matrix(heads)
    high, low = split_two(dd[...])
    dc = dot(collect, high, 1, 1) + dot(collect, low, 1, 1)
    b0 = dot(collect, pb[...], 1, 1)
    tail = running(dc, reverse=True)
    sig = 1.0 / (1.0 + jnp.exp(-raw[...]))
    over = sig / step
    turn = rate * sig
    vec_out[0] = b0 * over - turn * tail
    vec_out[1] = over
    vec_out[2] = turn
    vec_out[3] = step * leave
    vec_out[4] = jnp.broadcast_to(enter[:, length - 1 :], (heads, length))
    gm_out[:, :STATE] = dot(ms[...], maps[:, STATE:], 0, 0)
    gm_out[:, STATE:] = dot(ms[...], maps[:, :STATE], 1, 0) + dot(sc[...], sv, 1, 0)


def step_kernel(maps, carry, xl, states, vec, out, order):
    heads, length = vec.shape[1:]
    collect = gather_matrix(heads)
    both = carry[...].astype(f32) * states[...]
    inside = jnp.sum(both.reshape(heads, HEAD_DIM, STATE), axis=1)
    v = vec[4, :, 0:1] * jnp.sum(inside, axis=1, keepdims=True)
    got = []
    part = length // 4
    for d in range(4):
        rows = slice(d * part, (d + 1) * part)
        cb = dot(maps[rows, :STATE], carry[...], 1, 1)
        got.append(dot(collect, (xl[rows, :].astype(f32) * cb).astype(bf16), 1, 1))
    w = jnp.concatenate(got, axis=1)
    before = running(w) - w
    grad = vec[0] + w * vec[1] - vec[2] * (v + before)
    halves = [[], []]
    for c in range(order.shape[0]):
        order[c] = grad[:, c * 128 : (c + 1) * 128]
        for r in range(2):
            halves[r].append(order[c, pl.ds(r, heads // 2, stride=2), :])
    grad = jnp.concatenate([jnp.concatenate(h, axis=1) for h in halves], axis=0).astype(bf16)
    for k in range(out.shape[0]):
        out[k] = grad


def rest_kernel(maps, carry, xl, rdt, vec, gm, gx_out, gm_out):
    heads, length = vec.shape[1:]
    spread = spread_matrix(heads)
    scale = tall(vec[3])
    part = length // 4
    per = part // gm_out.shape[1]
    for d in range(4):
        rows = slice(d * part, (d + 1) * part)
        cb = dot(maps[rows, :STATE], carry[...], 1, 1)
        gx_out[rows, :] = (
            rdt[rows, :] + dot(scale[rows], spread, 1, 0) * cb
        ).astype(bf16)
        extra = gm[rows, :STATE] + dot(xl[rows, :], carry[...], 1, 0)
        size = part // per
        for k in range(per):
            inner = slice(k * size, (k + 1) * size)
            gm_out[d * per + k, :, :STATE] = extra[inner].astype(bf16)
            gm_out[d * per + k, :, STATE:] = gm[d * part + k * size : d * part + (k + 1) * size, STATE:].astype(bf16)


def project_kernel(grads, tokens, out, product, lined):
    groups, heads, length = grads.shape
    columns = tokens.shape[1]
    chunks = columns // 128
    half = heads // 2
    product[...] = dot(grads[...].reshape(groups * heads, length), tokens[...], 1, 0)
    for z in range(groups):
        for r in range(2):
            for c in range(chunks):
                lined[pl.ds(z * half * 2 * chunks + 2 * c + r, half, stride=2 * chunks), :] = (
                    product[z * heads + r * half : z * heads + (r + 1) * half, c * 128 : (c + 1) * 128]
                )
    out[...] = lined[...].astype(bf16).reshape(out.shape)


def total_kernel(pieces, sum_out, square_out):
    total = jnp.zeros(pieces.shape[1:], f32)
    for k in range(pieces.shape[0]):
        total = total + pieces[k].astype(f32)
    sum_out[...] = total
    square = total * total
    row = iota(total.shape, 0)
    first = jnp.sum(jnp.where(row % 2 == 0, square, 0.0), axis=(0, 1), keepdims=True)
    second = jnp.sum(jnp.where(row % 2 == 1, square, 0.0), axis=(0, 1), keepdims=True)
    shape = square_out.shape[1:]
    both = jnp.where(iota(shape, 0) % 2 == 0, first, second)
    for k in range(square_out.shape[0]):
        square_out[k] = both


def norm_kernel(squares, norm_out, pair_out):
    total = squares[0]
    for k in range(1, squares.shape[0]):
        total = total + squares[k]
    norm = jnp.sqrt(total + epsilon)
    norm_out[...] = norm
    pair = norm[0:1] + norm[1:2]
    for k in range(pair_out.shape[0]):
        pair_out[k] = pair


def clip_kernel(pairs, norm, summed, out):
    heads = 2 * pairs.shape[0]
    target = jnp.sum(pairs[...], axis=0) / heads
    scale = jnp.minimum(1.0, target / norm[...])
    for c in range(summed.shape[0] // 2):
        for r in range(2):
            k = 2 * c + r
            out[r : r + 1, c * 128 : (c + 1) * 128] = summed[k : k + 1, :] * scale[r : r + 1]


def call(kernel, outs, specs, flops, moved, scratch=(), limit=24, name=None):
    return pl.pallas_call(
        kernel,
        out_shape=outs,
        in_specs=specs,
        out_specs=jax.tree.map(lambda _: VMEM, outs),
        scratch_shapes=scratch,
        cost_estimate=pl.CostEstimate(flops=flops, bytes_accessed=moved, transcendentals=0),
        compiler_params=pltpu.CompilerParams(vmem_limit_bytes=limit << 20),
        name=name,
    )


def shards(x_in, grad_out, state_maps, dt_raw, a_log, saved_states, layer_in, doc_lengths):
    length, wide = x_in.shape[1:]
    heads = a_log.shape[0]
    x, dy, maps, raw = x_in[0], grad_out[0], state_maps[0], dt_raw[0]
    states = saved_states.reshape(wide, STATE)
    anchor = (lax.axis_index(CTX) * length).astype(jnp.int32).reshape(1)
    blocks = lax.axis_size(CTX)
    tp = lax.axis_size("tp")
    groups = lax.axis_size(DP_CTX)
    rows = wide // blocks
    SD = jax.ShapeDtypeStruct

    payload = call(
        first_kernel,
        SD((blocks, rows + 8, STATE), bf16),
        [SMEM, SMEM, SMEM, VMEM, VMEM, VMEM],
        200_000_000, 2_000_000, name="first",
    )(doc_lengths, anchor, a_log, raw, dy, maps)
    pieces = lax.all_to_all(payload, CTX, 0, 0, tiled=True)
    carries = call(
        scan_kernel, SD((blocks, rows, STATE), bf16), [VMEM], 1_000_000, 600_000, name="scan"
    )(pieces)
    carry = lax.all_to_all(carries, CTX, 0, 0, tiled=True).reshape(wide, STATE)

    big = lambda dtype: pltpu.VMEM((length, wide), dtype)
    rdt, xl, gm, vec = call(
        quad_kernel,
        (
            SD((length, wide), f32),
            SD((length, wide), bf16),
            SD((length, 2 * STATE), f32),
            SD((5, heads, length), f32),
        ),
        [SMEM, SMEM, SMEM, VMEM, VMEM, VMEM, VMEM, VMEM],
        4_000_000_000, 8_000_000,
        scratch=[
            *[big(bf16)] * 7,
            *[big(f32)] * 7,
            big(bf16),
            pltpu.VMEM((length, length), bf16),
            pltpu.VMEM((length, heads), f32),
            pltpu.VMEM((5, length, 2 * heads), bf16),
        ],
        limit=56, name="quad",
    )(doc_lengths, anchor, a_log, raw, x, dy, maps, states)

    grads = call(
        step_kernel,
        SD((tp, heads, length), bf16),
        [VMEM] * 5,
        300_000_000, 3_000_000,
        scratch=[pltpu.VMEM((length // 128, heads, 128), f32)],
        name="steps",
    )(maps, carry, xl, states, vec)
    gathered = lax.all_to_all(grads, "tp", 0, 0, tiled=True)
    grad_x, parts = call(
        rest_kernel,
        (SD((length, wide), bf16), SD((tp, length // tp, 2 * STATE), bf16)),
        [VMEM] * 6,
        400_000_000, 6_000_000, name="rest",
    )(maps, carry, xl, rdt, vec, gm)

    chunks = wide // 128
    partial = call(
        project_kernel,
        SD((groups, 2 * chunks, 128), bf16),
        [VMEM] * 2,
        200_000_000, 2_000_000,
        scratch=[pltpu.VMEM((tp * heads, wide), f32), pltpu.VMEM((groups * 2 * chunks, 128), f32)],
        name="project",
    )(gathered, layer_in[0])
    arrived = lax.all_to_all(partial, DP_CTX, 0, 0, tiled=True)
    maps_arrived = lax.all_to_all(parts, "tp", 0, 0, tiled=True)
    grad_maps = jnp.sum(maps_arrived.astype(f32), axis=0)

    summed, squares = call(
        total_kernel,
        (SD((2 * chunks, 128), f32), SD((tp, 8, 128), f32)),
        [VMEM],
        1_000_000, 300_000, name="total",
    )(arrived)
    squares = lax.all_to_all(squares, "tp", 0, 0, tiled=True)
    norm, pairs = call(
        norm_kernel,
        (SD((8, 128), f32), SD((groups, 1, 128), f32)),
        [VMEM],
        10_000, 70_000, name="norm",
    )(squares)
    pairs = lax.all_to_all(pairs, DP_CTX, 0, 0, tiled=True)
    grad_dt_proj = call(
        clip_kernel, SD((2, wide), f32), [VMEM] * 3, 10_000, 50_000, name="clip"
    )(pairs, norm, summed)
    return (grad_x[None], grad_maps[None], grad_dt_proj)


def solution(mesh):
    split = Mesh(
        mesh.devices.reshape(mesh.shape["dp"], 4, 8, mesh.shape["tp"]),
        ("dp", "ctx_0", "ctx_1", "tp"),
    )
    return jax.shard_map(
        shards,
        mesh=split,
        in_specs=(
            P("dp", CTX, "tp"),
            P("dp", CTX, "tp"),
            P("dp", CTX, None),
            P("dp", "tp", CTX),
            P("tp"),
            P("dp", CTX, "tp", None, None),
            P("dp", CTX, "tp"),
            P("dp", None),
        ),
        out_specs=(P("dp", CTX, "tp"), P("dp", CTX_TP, None), P(DP_CTX, "tp")),
        check_vma=False,
    )
```
